128 devices in a mesh: sub: 32 (over z, x, core), nar: 4 (over y).
Axes of the slice: x: 4, y: 4, z: 4, core: 2. Of those that a mesh axis runs over, the one named last changes fastest.
Arguments:
- remainder_inverse: bfloat16 [128, 2048, 2048], P(('sub', 'nar')), may hold values from -4 to 40, as said below
- dirichlet_schur: bfloat16 [128, 2048, 2048], P(('sub', 'nar')), may hold values from -4 to 40, as said below
- corner_coupling: bfloat16 [128, 24, 2048], P(('sub', 'nar')), may hold values from -0.125 to 0.125
- coarse_inverse: float32 [768, 768], replicated, may hold values from -4 to 40, as said below
- jump_load: float32 [107520, 256], P(('sub', 'nar')), may hold values from -40 to 40
- dof_multiplier: int32 [128, 2048], P(('sub', 'nar')), may hold values from 0 to 107519, as said below
- dof_sign: int32 [128, 2048], P(('sub', 'nar')), may hold values from -1 to 1
- corner_index: int32 [128, 24], P(('sub', 'nar')), may hold values from 0 to 767, as said below
Outputs:
- multipliers: float32 [107520, 256], P(('sub', 'nar'))
- residual: float32 [107520, 256], P(('sub', 'nar'))
The draws below stay inside these ranges and needn't reach their ends.
Inputs may be any that keep to these rules, and one draw needn't show every extreme that they name: Row m of the multipliers belongs to subdomain m // 840 and is named by exactly two entries of dof_multiplier: one in that subdomain's row and one in the row of another subdomain, with opposite nonzero signs in dof_sign. Writing a subdomain as 4 a + b, the other one is 4 a' + b' with a' one of a - 1, a, a + 1 modulo 128 // 4. An entry whose sign is 0 names no multiplier and holds 840 s for its subdomain s. Of one subdomain's 840 rows, the numbers held jointly with each of its 11 partners are, in an order drawn from the seed, 96 five times, 72 three times and 48 three times. `corner_index`: the 24 entries of one subdomain are distinct. `remainder_inverse`: each subdomain's matrix is symmetric positive definite. `dirichlet_schur`: each subdomain's matrix is symmetric positive definite. `coarse_inverse`: symmetric positive definite.
All inputs are finite; a program needn't handle non-finite values.
Results may differ from the reference program's by a relative error of at most 0.012.
The reference program's roundings to bfloat16 on the way count: a program that leaves them out, or rounds other values in their place, can miss the bound.
Values may be sent and summed in bfloat16 or wider, within the bound.
No kernel may reach another device: no remote copies, remote signals or barrier semaphores. Data moves between devices by JAX's collectives and lax.ppermute only.
A program may use at most 128 MiB of HBM per device.

```python
import jax
import jax.numpy as jnp
from jax import lax

NR = 2048
NCL = 24
CAP = 96
R = 256
ITERS = 2
SUBS = 128
NL_DEV = 840
NL = 107520
NCG = 768


def definite_block(seed_key, order, lowest, highest, spread):
    noise = jnp.clip(jax.random.normal(seed_key, (order, order), jnp.float32), -6.0, 6.0) * (spread / jnp.sqrt(jnp.float32(order)))
    symmetric = (noise + noise.T) * jnp.sqrt(jnp.float32(0.5))
    diagonal = jax.random.uniform(jax.random.fold_in(seed_key, 1), (order,), jnp.float32, lowest, highest)
    matrix = symmetric + jnp.diag(diagonal)
    return matrix


def draw_remainder_inverse(key, part):
    blocks = lax.map(lambda subdomain: definite_block(jax.random.fold_in(key, subdomain), NR, 1.0, 2.0, 0.4), jnp.arange(SUBS))
    return blocks.astype(jnp.bfloat16)


def draw_dirichlet_schur(key, part):
    blocks = lax.map(lambda subdomain: definite_block(jax.random.fold_in(key, subdomain + 100000), NR, 2.0, 4.0, 0.4), jnp.arange(SUBS))
    return blocks.astype(jnp.bfloat16)


def draw_coarse_inverse(key, part):
    return definite_block(jax.random.fold_in(key, 5), NCG, 2.0, 4.0, 0.5).astype(jnp.float32)


def draw_jump_load(key, part):
    base = jnp.clip(jax.random.normal(jax.random.fold_in(key, 21), (NL, R), jnp.float32), -6.0, 6.0)
    rise_base = 3.0
    column_scale = jnp.exp(jax.random.uniform(jax.random.fold_in(key, 22), (R,), jnp.float32, -1.15, 1.15))
    device_row = (jnp.arange(NL) // NL_DEV).astype(jnp.float32)
    fraction = device_row / jnp.float32(SUBS - 1) - 0.5
    rise = jnp.power(jnp.float32(rise_base), fraction)
    values = base * column_scale[None, :] * rise[:, None]
    return values.astype(jnp.float32)


def build_routing(seed_key):
    count_sub = SUBS // 4
    base_counts = jnp.array([CAP] * 5 + [3 * CAP // 4] * 3 + [CAP // 2] * 3, jnp.int32)
    subdomain = jnp.arange(SUBS, dtype=jnp.int32)
    order_keys = jax.random.split(jax.random.fold_in(seed_key, 1), SUBS)
    chosen = jax.vmap(lambda one_key: jax.random.permutation(one_key, 11).astype(jnp.int32))(order_keys)
    counts = base_counts[chosen]
    peer_rank = jnp.arange(11, dtype=jnp.int32)[None, :]
    classes = peer_rank + (peer_rank >= (4 + subdomain % 4)[:, None]).astype(jnp.int32)
    peers = (subdomain[:, None] // 4 + classes // 4 - 1) % count_sub * 4 + classes % 4
    bounds = jnp.cumsum(counts, axis=1)
    position = jnp.arange(NL_DEV, dtype=jnp.int32)
    peer_slot = jnp.sum((position[None, :, None] >= bounds[:, None, :]).astype(jnp.int32), axis=2)
    shuffle_keys = jax.random.split(jax.random.fold_in(seed_key, 2), SUBS)
    shuffled = jax.vmap(lambda one_key, row_slots: row_slots[jax.random.permutation(one_key, NL_DEV).astype(jnp.int32)])(shuffle_keys, peer_slot)
    partner = jnp.take_along_axis(peers, shuffled, axis=1).reshape(-1).astype(jnp.int32)
    owner_sign = (2 * jax.random.randint(jax.random.fold_in(seed_key, 3), (SUBS * NL_DEV,), 0, 2) - 1).astype(jnp.int32)
    sorter = jnp.argsort(partner, stable=True).astype(jnp.int32)
    sorted_partner = partner[sorter]
    starts = jnp.searchsorted(sorted_partner, subdomain).astype(jnp.int32)
    arrival = jnp.zeros_like(partner).at[sorter].set(jnp.arange(SUBS * NL_DEV, dtype=jnp.int32) - starts[sorted_partner])
    dof_keys = jax.random.split(jax.random.fold_in(seed_key, 4), SUBS)
    layout = jax.vmap(lambda one_key: jax.random.permutation(one_key, NR).astype(jnp.int32))(dof_keys)
    multiplier = jnp.arange(SUBS * NL_DEV, dtype=jnp.int32)
    holder = multiplier // NL_DEV
    own_place = holder * NR + layout[holder, multiplier % NL_DEV]
    far_place = partner * NR + layout[partner, NL_DEV + arrival]
    targets = jnp.repeat(subdomain * NL_DEV, NR).at[own_place].set(multiplier).at[far_place].set(multiplier)
    signs = jnp.zeros((SUBS * NR,), jnp.int32).at[own_place].set(owner_sign).at[far_place].set(-owner_sign)
    return (targets.reshape(SUBS, NR).astype(jnp.int32), signs.reshape(SUBS, NR).astype(jnp.int32))


def draw_dof_multiplier(key, part):
    return build_routing(jax.random.fold_in(key, 7))[0]


def draw_dof_sign(key, part):
    return build_routing(jax.random.fold_in(key, 7))[1]


def draw_corner_index(key, part):
    row_keys = jax.random.split(jax.random.fold_in(key, 9), SUBS)
    picks = jax.vmap(lambda one_key: jax.random.permutation(one_key, NCG)[:NCL].astype(jnp.int32))(row_keys)
    return picks.astype(jnp.int32)


def steps_of(rng, shape, pieces, smallest, high):
    def one(dim, blocks):
        draws = jax.random.uniform(jax.random.fold_in(jax.random.fold_in(rng, 6), dim), (blocks,), jnp.float32, smallest / len(pieces), high / len(pieces))
        return jnp.repeat(jnp.exp(draws), shape[dim] // blocks).reshape((-1,) + (1,) * (len(shape) - dim - 1))

    level = one(*pieces[0])
    for cut in pieces[1:]:
        level = level * one(*cut)
    return level


def scatter_about(stream_key, shape, deviation, most, shards=(), kind=jnp.bfloat16):
    loudness = steps_of(stream_key, shape, shards, -0.22, 0.18) if shards else 1.0
    entries = jax.random.normal(stream_key, shape, jnp.float32) * deviation * loudness
    return jnp.minimum(jnp.maximum(entries, -most), most).astype(kind)


def setup_inputs(seed: int = 0) -> dict:
    keys = jax.random.split(jax.random.key(seed), 9)
    remainder_inverse = draw_remainder_inverse(jax.random.fold_in(keys[8], 71), 0)
    dirichlet_schur = draw_dirichlet_schur(jax.random.fold_in(keys[8], 71), 0)
    corner_coupling = scatter_about(keys[2], (SUBS, NCL, NR), NR ** -0.5, 0.125, ((0, 128),))
    coarse_inverse = draw_coarse_inverse(jax.random.fold_in(keys[8], 71), 0)
    jump_load = draw_jump_load(jax.random.fold_in(keys[8], 71), 0)
    dof_multiplier = draw_dof_multiplier(jax.random.fold_in(keys[8], 71), 0)
    dof_sign = draw_dof_sign(jax.random.fold_in(keys[8], 71), 0)
    corner_index = draw_corner_index(jax.random.fold_in(keys[8], 71), 0)
    return dict(remainder_inverse=remainder_inverse, dirichlet_schur=dirichlet_schur, corner_coupling=corner_coupling, coarse_inverse=coarse_inverse, jump_load=jump_load, dof_multiplier=dof_multiplier, dof_sign=dof_sign, corner_index=corner_index)


def signed_rows(vector, dof_multiplier, dof_sign):
    picked = vector[dof_multiplier] * dof_sign.astype(jnp.float32)[:, :, None]
    return picked.astype(jnp.bfloat16)


def signed_sum(terms, dof_multiplier, dof_sign, row_count):
    weighted = terms.astype(jnp.float32) * dof_sign.astype(jnp.float32)[:, :, None]
    width_cols = terms.shape[2]
    return jnp.zeros((row_count, width_cols), jnp.float32).at[dof_multiplier.reshape(-1)].add(weighted.reshape(-1, width_cols))


def each_product(matrices, operands):
    return lax.map(lambda paired: jnp.dot(paired[0], paired[1], preferred_element_type=jnp.float32), (matrices, operands))


def each_transposed(matrices, operands):
    return lax.map(lambda paired: jnp.dot(paired[0].T, paired[1], preferred_element_type=jnp.float32), (matrices, operands))


def reference(remainder_inverse, dirichlet_schur, corner_coupling, coarse_inverse, jump_load, dof_multiplier, dof_sign, corner_index):
    row_count = jump_load.shape[0]
    columns = jump_load.shape[1]

    def flexibility(vector):
        jumped = signed_rows(vector, dof_multiplier, dof_sign)
        local_part = each_product(remainder_inverse, jumped)
        corner_part = each_product(corner_coupling, jumped)
        coarse_load = jnp.zeros((NCG, columns), jnp.float32).at[corner_index.reshape(-1)].add(corner_part.reshape(-1, columns))
        picked = coarse_inverse[corner_index]
        coarse_solution = jnp.einsum("snc,cr->snr", picked, coarse_load, precision=lax.Precision.HIGHEST).astype(jnp.bfloat16)
        summed = (local_part + each_transposed(corner_coupling, coarse_solution)).astype(jnp.bfloat16)
        return signed_sum(summed, dof_multiplier, dof_sign, row_count)

    def precondition(vector):
        jumped = signed_rows(vector, dof_multiplier, dof_sign)
        stiff_rows = each_product(dirichlet_schur, jumped).astype(jnp.bfloat16)
        return signed_sum(stiff_rows, dof_multiplier, dof_sign, row_count)

    residual = jump_load
    multipliers = jnp.zeros_like(jump_load)
    reduced = precondition(residual)
    energy = jnp.sum(residual * reduced, axis=0)
    direction = reduced
    for iteration in range(ITERS):
        product_rows = flexibility(direction)
        step_size = energy / jnp.sum(direction * product_rows, axis=0)
        multipliers = multipliers + step_size * direction
        residual = residual - step_size * product_rows
        if iteration + 1 < ITERS:
            reduced = precondition(residual)
            energy_later = jnp.sum(residual * reduced, axis=0)
            direction = reduced + (energy_later / energy) * direction
            energy = energy_later
    return multipliers, residual
```

```python
import functools

import jax
import jax.numpy as jnp
from jax import lax
from jax.experimental import pallas as pl
from jax.experimental.pallas import tpu as pltpu
from jax.sharding import PartitionSpec as P

CAP = 96
SLAB = 2 * CAP
NAR = 4
AXES = ("sub", "nar")
PEERS = [(da, db) for da in (-1, 0, 1) for db in range(NAR) if (da, db) != (0, 0)]
COUNT = len(PEERS)
FAR_KEY = 1000
CHUNKS = 4
BF = jnp.bfloat16
F32 = jnp.float32
VMEM_LIMIT = 60 * 1024 * 1024


def mirror(p):
    da, db = PEERS[p]
    return PEERS.index((-da, -db % NAR))


def peer_pairs(p, subs):
    da, db = PEERS[p]
    return [
        (a * NAR + b, (a + da) % subs * NAR + (b + db) % NAR)
        for a in range(subs)
        for b in range(NAR)
    ]


def swap_pairs(kind, subs):
    def other(a, b):
        z, x, core = a // 8, a // 2 % 4, a % 2
        if kind == "core":
            core ^= 1
        elif kind == "x1":
            x ^= 1
        elif kind == "x3":
            x = 3 - x
        elif kind == "z1":
            z ^= 1
        elif kind == "z3":
            z = 3 - z
        elif kind == "y1":
            b ^= 1
        elif kind == "y3":
            b = 3 - b
        return (z * 8 + x * 2 + core) * NAR + b

    return [(a * NAR + b, other(a, b)) for a in range(subs) for b in range(NAR)]


def exchange(slabs):
    subs = lax.axis_size("sub")
    got = [None] * COUNT
    for p in range(COUNT):
        got[mirror(p)] = lax.ppermute(slabs[p], AXES, peer_pairs(p, subs))
    return got


def swapped(block, kind):
    return lax.ppermute(block, AXES, swap_pairs(kind, lax.axis_size("sub")))


def all_sum(block):
    for kind in ("core", "y1", "y3", "x1", "x3", "z1", "z3"):
        block = block + swapped(block, kind)
    return block


def line_gather(block):
    for kind in ("core", "x1", "x3", "z1"):
        block = jnp.concatenate([block, swapped(block, kind)], axis=0)
    return block, swapped(block, "z3")


def split3(value):
    high = value.astype(BF)
    rest = value - high.astype(F32)
    middle = rest.astype(BF)
    low = (rest - middle.astype(F32)).astype(BF)
    return high, middle, low


def dot(left, right):
    return jnp.dot(left, right, preferred_element_type=F32)


def big_copy(source, target, sems):
    rows = source.shape[0] // CHUNKS
    copies = []
    for i in range(CHUNKS):
        part = pl.ds(i * rows, rows)
        copies.append(pltpu.make_async_copy(source.at[part, :], target.at[part, :], sems.at[i]))
    return copies


def product_loop(matrix, operand, copies, sink):
    rows = matrix.shape[0] // CHUNKS
    for i in range(CHUNKS):
        copies[i].wait()
        part = pl.ds(i * rows, rows)
        sink(part, dot(matrix[part, :], operand[...]))


def start_kernel(wanted_ref, jump_ref, *outs):
    high, middle, low = split3(jump_ref[...])
    rows = jump_ref.shape[0]
    for p in range(COUNT):
        names = wanted_ref[p * CAP : (p + 1) * CAP, :]
        pick = (lax.broadcasted_iota(jnp.int32, (CAP, rows), 1) + 1 == names).astype(F32).astype(BF)
        outs[p][...] = dot(pick, high) + dot(pick, middle) + dot(pick, low)


def slots_of(p):
    own = slice(p * SLAB, p * SLAB + CAP)
    far = slice(p * SLAB + CAP, (p + 1) * SLAB)
    return own, far


def schur_kernel(first, *refs):
    refs = list(refs)
    take = lambda n: [refs.pop(0) for _ in range(n)]
    own0, far0 = take(COUNT), take(COUNT)
    if not first:
        mine, theirs = take(COUNT), take(COUNT)
        energy_ref, curve_ref = take(2)
    spread_hbm, schur_hbm, slots_hbm = take(3)
    outs = take(COUNT)
    (energy_out,) = take(1)
    if not first:
        (residual_out,) = take(1)
    spread_v, schur_v, slots_v, value, jump, dofs, product, slot_product, sems = refs
    spread_copies = big_copy(spread_hbm, spread_v, sems.at[0])
    schur_copies = big_copy(schur_hbm, schur_v, sems.at[1])
    slots_copies = big_copy(slots_hbm, slots_v, sems.at[2])
    for copy in spread_copies + schur_copies + slots_copies:
        copy.start()
    if not first:
        step = energy_ref[0:1, :] / curve_ref[0:1, :]
    for p in range(COUNT):
        own, far = slots_of(p)
        own_value = own0[p][...]
        far_value = far0[p][...]
        if not first:
            top, bottom = mine[p][0:CAP, :].astype(F32), mine[p][CAP:SLAB, :].astype(F32)
            own_value = own_value - step * (top + theirs[p][CAP:SLAB, :].astype(F32))
            far_value = far_value - step * (bottom + theirs[p][0:CAP, :].astype(F32))
            residual_out[p * CAP : (p + 1) * CAP, :] = own_value
        value[own, :] = own_value
        value[far, :] = far_value
        jump[own, :] = own_value.astype(BF)
        jump[far, :] = far_value.astype(BF)

    def put(target):
        def sink(part, result):
            target[part, :] = result.astype(BF)

        return sink

    product_loop(spread_v, jump, spread_copies, put(dofs))
    product_loop(schur_v, dofs, schur_copies, put(product))
    product_loop(slots_v, product, slots_copies, put(slot_product))
    total = jnp.zeros((8, value.shape[1]), F32)
    for p in range(COUNT):
        part = slice(p * SLAB, (p + 1) * SLAB)
        block = slot_product[part, :]
        outs[p][...] = block
        terms = value[part, :] * block.astype(F32)
        total = total + jnp.sum(terms.reshape(SLAB // 8, 8, -1), axis=0)
    energy_out[...] = jnp.broadcast_to(jnp.sum(total, axis=0, keepdims=True), total.shape)


def jump_kernel(wide, *refs):
    refs = list(refs)
    take = lambda n: [refs.pop(0) for _ in range(n)]
    mine, theirs = take(COUNT), take(COUNT)
    energy_ref, coupling_ref = take(2)
    if wide:
        (names_ref,) = take(1)
    (spread_hbm,) = take(1)
    dofs_out, coarse_out, direction_out = take(3)
    spread_v, jump, sems = refs
    copies = big_copy(spread_hbm, spread_v, sems.at[0])
    for copy in copies:
        copy.start()
    for p in range(COUNT):
        own, far = slots_of(p)
        top, bottom = mine[p][0:CAP, :].astype(F32), mine[p][CAP:SLAB, :].astype(F32)
        own_value = top + theirs[p][CAP:SLAB, :].astype(F32)
        far_value = bottom + theirs[p][0:CAP, :].astype(F32)
        direction_out[own, :] = own_value
        direction_out[far, :] = far_value
        jump[own, :] = own_value.astype(BF)
        jump[far, :] = far_value.astype(BF)

    def sink(part, result):
        dofs_out[part, :] = result.astype(BF)

    product_loop(spread_v, jump, copies, sink)
    corner = dot(coupling_ref[...], dofs_out[...])
    energy = energy_ref[0:1, :]
    high, middle, low = split3(energy)
    extra = jnp.concatenate(
        [high.astype(F32), middle.astype(F32), low.astype(F32), jnp.zeros((5, energy.shape[1]), F32)],
        axis=0,
    )
    rows = jnp.concatenate([corner, extra], axis=0)
    if wide:
        rows = jnp.concatenate([rows, names_ref[...]], axis=1)
    coarse_out[...] = rows.astype(BF)


def local_kernel(inverse_hbm, dofs_ref, out, inverse_v, sems):
    copies = big_copy(inverse_hbm, inverse_v, sems.at[0])
    for copy in copies:
        copy.start()

    def sink(part, result):
        out[part, :] = result

    product_loop(inverse_v, dofs_ref, copies, sink)


def coarse_kernel(first, *refs):
    if first:
        left, right, rows_ref, out, select_out = refs
        half = left.shape[0]
        columns = left.shape[1] - 128
        high, middle, low = split3(rows_ref[...])
        size = rows_ref.shape[1]
        contract = (((1,), (1,)), ((), ()))
        parts = []
        for ref in (left, right):
            names = ref[:, columns : columns + 128].astype(F32)
            index = (names[:, 0:1] * 32.0 + names[:, 1:2]).astype(jnp.int32)
            pick = lax.broadcasted_iota(jnp.int32, (half, size), 1) == index
            pick = pick.astype(F32).astype(BF)
            part = sum(
                lax.dot_general(piece, pick, contract, preferred_element_type=F32)
                for piece in (high, middle, low)
            )
            row = lax.broadcasted_iota(jnp.int32, part.shape, 0) % 32
            lane = lax.broadcasted_iota(jnp.int32, part.shape, 1) % 32
            energy = (lane >= 24) & (lane < 27)
            part = jnp.where(row < 24, part, jnp.where((row == 24) & energy, 1.0, 0.0))
            parts.append(part)
        select = jnp.concatenate(parts, axis=1)
        select_out[...] = select
    else:
        left, right, select_ref, out = refs
        half = left.shape[0]
        columns = left.shape[1]
        select = select_ref[...]
    total = None
    for i, ref in enumerate((left, right)):
        block = ref[:, 0:columns]
        for piece in split3(select[:, i * half : (i + 1) * half]):
            term = dot(piece, block)
            total = term if total is None else total + term
    out[...] = total


def flex_kernel(first, *refs):
    refs = list(refs)
    take = lambda n: [refs.pop(0) for _ in range(n)]
    parts = take(4)
    local_ref, coupling_ref, direction_ref = take(3)
    if not first:
        before_ref, energy_ref, old_direction_ref = take(3)
    (slots_hbm,) = take(1)
    outs = take(COUNT)
    if not first:
        keeps = take(COUNT)
    energy_out, curve_out = take(2)
    if first:
        (before_out,) = take(1)
    slots_v, product, slot_product, sems = refs
    copies = big_copy(slots_hbm, slots_v, sems.at[0])
    for copy in copies:
        copy.start()
    coarse = parts[0][...] + parts[1][...] + parts[2][...] + parts[3][...]
    energy_out[...] = jnp.broadcast_to(coarse[24:25, :], energy_out.shape)
    solution_rows = coarse[0:24, :].astype(BF)
    back = lax.dot_general(
        coupling_ref[...],
        solution_rows,
        (((0,), (0,)), ((), ())),
        preferred_element_type=F32,
    )
    whole = local_ref[...] + back
    if first:
        before_out[...] = whole
        ratio = None
    else:
        ratio = coarse[24:25, :] / energy_ref[0:1, :]
        whole = whole + ratio * before_ref[...]
    product[...] = whole.astype(BF)

    def sink(part, result):
        slot_product[part, :] = result.astype(BF)

    product_loop(slots_v, product, copies, sink)
    total = jnp.zeros((8, whole.shape[1]), F32)
    for p in range(COUNT):
        part = slice(p * SLAB, (p + 1) * SLAB)
        own, far = slots_of(p)
        block = slot_product[part, :]
        if first:
            outs[p][...] = block
        else:
            keeps[p][...] = slot_product[own, :]
            outs[p][...] = slot_product[far, :]
        direction = direction_ref[part, :]
        if not first:
            direction = direction + ratio * old_direction_ref[part, :]
        terms = direction * block.astype(F32)
        total = total + jnp.sum(terms.reshape(SLAB // 8, 8, -1), axis=0)
    curve_out[...] = jnp.broadcast_to(jnp.sum(total, axis=0, keepdims=True), total.shape)


def final_kernel(*refs):
    refs = list(refs)
    take = lambda n: [refs.pop(0) for _ in range(n)]
    keeps, gots = take(COUNT), take(COUNT)
    residual_ref, old_ref, new_ref, wanted_ref = take(4)
    e0, c0, e1, c1 = [ref[0:1, :] for ref in take(4)]
    multipliers_out, residual_out = take(2)
    owned = multipliers_out.shape[0]
    step0 = e0 / c0
    step1 = e1 / c1
    ratio = e1 / e0
    xs, rs = [], []
    for p in range(COUNT):
        own, _ = slots_of(p)
        old = old_ref[own, :]
        direction = new_ref[own, :] + ratio * old
        image = keeps[p][...].astype(F32) + gots[p][...].astype(F32)
        xs.append(step0 * old + step1 * direction)
        rs.append(residual_ref[p * CAP : (p + 1) * CAP, :] - step1 * image)
    names = wanted_ref[...]
    pick = lax.broadcasted_iota(jnp.int32, (owned, names.shape[1]), 0) + 1 == names
    pick = pick.astype(F32).astype(BF)
    for blocks, out in ((xs, multipliers_out), (rs, residual_out)):
        total = None
        for piece in split3(jnp.concatenate(blocks, axis=0)):
            term = dot(pick, piece)
            total = term if total is None else total + term
        out[...] = total


VM = pl.BlockSpec(memory_space=pltpu.VMEM)
HBM = pl.BlockSpec(memory_space=pl.ANY)


def call(kernel, inputs, in_hbm, outs, scratch, flops, name):
    specs = [VM] * len(inputs) + [HBM] * len(in_hbm)
    moved = sum(x.size * x.dtype.itemsize for x in list(inputs) + list(in_hbm))
    return pl.pallas_call(
        kernel,
        out_shape=[jax.ShapeDtypeStruct(s, d) for s, d in outs],
        in_specs=specs,
        out_specs=[VM] * len(outs),
        scratch_shapes=scratch,
        compiler_params=pltpu.CompilerParams(vmem_limit_bytes=VMEM_LIMIT),
        cost_estimate=pl.CostEstimate(flops=flops, bytes_accessed=moved, transcendentals=0),
        name=name,
    )(*inputs, *in_hbm)


def routing(targets, signs, corners, owned):
    subs = lax.axis_size("sub")
    a = lax.axis_index("sub")
    b = lax.axis_index("nar")
    me = a * NAR + b
    count = targets.shape[0]
    holder = targets // owned
    row = targets - holder * owned
    linked = signs != 0
    home = linked & (holder == me)
    remote = linked & (holder != me)
    kind = (holder // NAR - a + 1) % subs * NAR + (holder % NAR - b) % NAR
    peer = jnp.where(remote, kind - (kind > NAR), COUNT)
    blocks = count // 128
    lanes = peer.reshape(blocks, 128).T
    member = lanes[:, :, None] == jnp.arange(16)[None, None, :]
    member = member.astype(F32).reshape(128, blocks * 16)
    before = jnp.arange(128)[:, None] > jnp.arange(128)[None, :]
    within = dot(before.astype(BF), member.astype(BF)).reshape(128, blocks, 16)
    totals = jnp.sum(member, axis=0).reshape(blocks, 16)
    ahead = jnp.arange(blocks)[:, None] > jnp.arange(blocks)[None, :]
    base = jnp.sum(ahead.astype(F32)[:, :, None] * totals[None, :, :], axis=1)
    rank = jnp.sum(member.reshape(128, blocks, 16) * (within + base[None, :, :]), axis=2)
    rank = rank.T.reshape(count).astype(jnp.int32)
    place = peer * CAP + rank
    far_names = jnp.arange(COUNT * CAP)
    hit = jnp.where(remote, place, -1)[:, None] == far_names[None, :]
    request = jnp.max(jnp.where(hit, (row + 1)[:, None], 0), axis=0).reshape(COUNT, CAP)
    message = jnp.concatenate(
        [
            request,
            jnp.broadcast_to(corners[None, :], (COUNT, corners.shape[0])),
            jnp.zeros((COUNT, 128 - CAP - corners.shape[0]), jnp.int32),
        ],
        axis=1,
    )
    got = jnp.concatenate(exchange([message[p : p + 1, :] for p in range(COUNT)]), axis=0)
    wanted = got[:, :CAP]
    dof_key = jnp.where(home, row + 1, jnp.where(remote, FAR_KEY + place, -2))
    slot_key = jnp.concatenate(
        [jnp.where(wanted > 0, wanted, -1), FAR_KEY + far_names.reshape(COUNT, CAP)], axis=1
    ).reshape(COUNT * SLAB)
    slots = jnp.where(slot_key[:, None] == dof_key[None, :], signs[None, :], 0)
    spread = jnp.where(dof_key[:, None] == slot_key[None, :], signs[:, None], 0)
    mates = [corners] + [
        got[PEERS.index((0, db)), CAP : CAP + corners.shape[0]] for db in range(1, NAR)
    ]
    mates = jnp.concatenate(
        [jnp.pad(names, (0, 32 - names.shape[0])) for names in mates], axis=0
    )
    return wanted.reshape(COUNT * CAP), slots.astype(BF), spread.astype(BF), mates


def body(
    remainder_inverse,
    dirichlet_schur,
    corner_coupling,
    coarse_inverse,
    jump_load,
    dof_multiplier,
    dof_sign,
    corner_index,
):
    inverse = remainder_inverse[0]
    schur = dirichlet_schur[0]
    coupling = corner_coupling[0]
    corners = corner_index[0]
    owned, columns = jump_load.shape
    dofs_n = inverse.shape[0]
    slots_n = COUNT * SLAB
    wanted, slots, spread, mates = routing(dof_multiplier[0], dof_sign[0], corners, owned)
    coarse_rows = coarse_inverse[mates]
    names = jnp.pad(corners, (0, 32 - corners.shape[0]), constant_values=1023)
    names = jnp.stack([names // 32, names % 32], axis=1).astype(F32)
    names = jnp.pad(names, ((0, 0), (0, 126)))

    small = ((8, columns), F32)
    slab_outs = [((SLAB, columns), BF)] * COUNT
    half_outs = [((CAP, columns), BF)] * COUNT
    spread_v = pltpu.VMEM((dofs_n, slots_n), BF)
    square_v = pltpu.VMEM((dofs_n, dofs_n), BF)
    slots_v = pltpu.VMEM((slots_n, dofs_n), BF)
    slot_f = pltpu.VMEM((slots_n, columns), F32)
    slot_b = pltpu.VMEM((slots_n, columns), BF)
    dof_b = pltpu.VMEM((dofs_n, columns), BF)
    sems = lambda n: pltpu.SemaphoreType.DMA((n, CHUNKS))
    one = 2 * dofs_n * slots_n * columns

    own0 = call(
        start_kernel,
        [wanted[:, None], jump_load],
        [],
        [((CAP, columns), F32)] * COUNT,
        [],
        6 * COUNT * CAP * owned * columns,
        "start",
    )
    far0 = exchange(own0)

    def precondition(first, extra):
        return call(
            functools.partial(schur_kernel, first),
            [*own0, *far0, *extra],
            [spread, schur, slots],
            slab_outs + [small] + ([] if first else [((COUNT * CAP, columns), F32)]),
            [spread_v, square_v, slots_v, slot_f, slot_b, dof_b, dof_b, slot_b, sems(3)],
            3 * one,
            "schur",
        )

    def jumped(mine, theirs, energy, wide):
        return call(
            functools.partial(jump_kernel, wide),
            [*mine, *theirs, energy, coupling] + ([names] if wide else []),
            [spread],
            [
                ((dofs_n, columns), BF),
                ((32, columns + (128 if wide else 0)), BF),
                ((slots_n, columns), F32),
            ],
            [spread_v, slot_b, sems(1)],
            one,
            "jump",
        )

    def local(dofs):
        return call(
            local_kernel, [dofs], [], [((dofs_n, columns), F32)], [square_v, sems(1)], one, "local"
        )

    def local_product(dofs):
        return pl.pallas_call(
            local_kernel,
            out_shape=jax.ShapeDtypeStruct((dofs_n, columns), F32),
            in_specs=[HBM, VM],
            out_specs=VM,
            scratch_shapes=[square_v, sems(1)],
            compiler_params=pltpu.CompilerParams(vmem_limit_bytes=VMEM_LIMIT),
            cost_estimate=pl.CostEstimate(
                flops=one, bytes_accessed=2 * dofs_n * dofs_n, transcendentals=0
            ),
            name="local",
        )(inverse, dofs)

    def mate_sum(parts):
        subs = lax.axis_size("sub")
        got = [parts[0:32]]
        for db in range(1, NAR):
            p = PEERS.index((0, db))
            got.append(lax.ppermute(parts[32 * db : 32 * db + 32], AXES, peer_pairs(p, subs)))
        return got

    *reduced, energy_part = precondition(True, [])
    reduced_got = exchange(reduced)
    dofs, coarse_part, direction = jumped(reduced, reduced_got, energy_part, True)
    left, right = line_gather(coarse_part)
    local_rows = local_product(dofs)
    parts, select = call(
        functools.partial(coarse_kernel, True),
        [left, right, coarse_rows],
        [],
        [((128, columns), F32), ((128, 1024), F32)],
        [],
        10**9,
        "coarse",
    )
    *image, energy0, curve_part, before = call(
        functools.partial(flex_kernel, True),
        [*mate_sum(parts), local_rows, coupling, direction],
        [slots],
        slab_outs + [small, small, ((dofs_n, columns), F32)],
        [slots_v, dof_b, slot_b, sems(1)],
        one,
        "flex",
    )
    image_got = exchange(image)
    curve0 = all_sum(curve_part)

    *reduced, energy_part, residual1 = precondition(
        False, [*image, *image_got, energy0, curve0]
    )
    reduced_got = exchange(reduced)
    dofs, coarse_part, direction1 = jumped(reduced, reduced_got, energy_part, False)
    left, right = line_gather(coarse_part)
    local_rows = local_product(dofs)
    (parts,) = call(
        functools.partial(coarse_kernel, False),
        [left, right, select],
        [],
        [((128, columns), F32)],
        [],
        10**9,
        "coarse",
    )
    flexed = call(
        functools.partial(flex_kernel, False),
        [*mate_sum(parts), local_rows, coupling, direction1, before, energy0, direction],
        [slots],
        half_outs + half_outs + [small, small],
        [slots_v, dof_b, slot_b, sems(1)],
        one,
        "flex",
    )
    sent, kept = flexed[:COUNT], flexed[COUNT : 2 * COUNT]
    energy1, curve_part = flexed[2 * COUNT :]
    got = exchange(sent)
    curve1 = all_sum(curve_part)
    return tuple(
        call(
            final_kernel,
            [*kept, *got, residual1, direction, direction1, wanted[None, :]]
            + [energy0, curve0, energy1, curve1],
            [],
            [((owned, columns), F32)] * 2,
            [],
            12 * COUNT * CAP * owned * columns,
            "final",
        )
    )


def solution(mesh):
    placed = (
        P(AXES, None, None),
        P(AXES, None, None),
        P(AXES, None, None),
        P(),
        P(AXES, None),
        P(AXES, None),
        P(AXES, None),
        P(AXES, None),
    )
    return jax.shard_map(
        body,
        mesh=mesh,
        in_specs=placed,
        out_specs=(P(AXES, None), P(AXES, None)),
        check_vma=False,
    )
```

```python
import functools

import jax
import jax.numpy as jnp
from jax import lax
from jax.experimental import pallas as pl
from jax.experimental.pallas import tpu as pltpu
from jax.sharding import PartitionSpec as P


CAP = 96
SLAB = 2 * CAP
NAR = 4
AXES = ("sub", "nar")
PEERS = [(da, db) for da in (-1, 0, 1) for db in range(NAR) if (da, db) != (0, 0)]
COUNT = len(PEERS)
ORDER = [PEERS.index(p) for p in ((1, 0), (-1, 0), (0, 1), (0, 3), (0, 2))] + [
    PEERS.index((da, db)) for db in (1, 3, 2) for da in (1, -1)
]
FAR_KEY = 1000
CHUNKS = 4
DOFS = 2048
BF = jnp.bfloat16
F32 = jnp.float32
VMEM_LIMIT = 60 * 1024 * 1024


def mirror(p):
    da, db = PEERS[p]
    return PEERS.index((-da, -db % NAR))


def peer_pairs(p, subs):
    da, db = PEERS[p]
    return [
        (a * NAR + b, (a + da) % subs * NAR + (b + db) % NAR)
        for a in range(subs)
        for b in range(NAR)
    ]


def swap_pairs(kind, subs):
    def other(a, b):
        z, x, core = a // 8, a // 2 % 4, a % 2
        if kind == "core":
            core ^= 1
        elif kind == "x1":
            x ^= 1
        elif kind == "x3":
            x = 3 - x
        elif kind == "z1":
            z ^= 1
        elif kind == "z3":
            z = 3 - z
        elif kind == "y1":
            b ^= 1
        elif kind == "y3":
            b = 3 - b
        return (z * 8 + x * 2 + core) * NAR + b

    return [(a * NAR + b, other(a, b)) for a in range(subs) for b in range(NAR)]


def exchange(slabs):
    subs = lax.axis_size("sub")
    got = [None] * COUNT
    for p in ORDER:
        got[mirror(p)] = lax.ppermute(slabs[p], AXES, peer_pairs(p, subs))
    return got


def shifted(block, axis, by):
    subs = lax.axis_size("sub")

    def other(a, b):
        z, x, core = a // 8, a // 2 % 4, a % 2
        if axis == "z":
            z = (z + by) % 4
        elif axis == "x":
            x = (x + by) % 4
        else:
            b = (b + by) % NAR
        return (z * 8 + x * 2 + core) * NAR + b

    pairs = [(a * NAR + b, other(a, b)) for a in range(subs) for b in range(NAR)]
    return lax.ppermute(block, AXES, pairs)


def swapped(block, kind):
    return lax.ppermute(block, AXES, swap_pairs(kind, lax.axis_size("sub")))


def after(block, gate):
    return lax.optimization_barrier((block, gate))[0]


SUM_KINDS = ("core", "y1", "y3", "x1", "x3", "z1", "z3")


def exchange_and_sum(slabs, block):
    subs = lax.axis_size("sub")
    got = [None] * COUNT
    for p in ORDER:
        got[mirror(p)] = lax.ppermute(slabs[p], AXES, peer_pairs(p, subs))
    for kind in SUM_KINDS:
        arrived = swapped(block, kind)
        block = block + arrived
    return got, block


def routed_exchange(messages):
    subs = lax.axis_size("sub")
    index = PEERS.index
    one = lambda da: [(a * NAR + b, (a + da) % subs * NAR + b) for a in range(subs) for b in range(NAR)]
    bundle = lambda da: jnp.concatenate([messages[index((da, db))] for db in range(NAR)], axis=0)
    low = lax.ppermute(bundle(1), AXES, one(1))
    high = lax.ppermute(bundle(-1), AXES, one(-1))
    got = [None] * COUNT
    got[index((-1, 0))] = low[0:1]
    got[index((1, 0))] = high[0:1]
    for db in range(1, NAR):
        pack = jnp.concatenate(
            [messages[index((0, db))], low[db : db + 1], high[db : db + 1]], axis=0
        )
        arrived = shifted(pack, "y", db)
        back = -db % NAR
        for i, da in enumerate((0, -1, 1)):
            got[index((da, back))] = arrived[i : i + 1]
    return got


def line_gather(block, gate):
    rows = [block] + [shifted(block, "x", k) for k in (1, 3, 2)]
    plane = jnp.concatenate(rows, axis=0)
    planes = [plane] + [shifted(plane, "z", k) for k in (1, 3, 2)]
    planes[3] = after(planes[3], gate)
    return planes + [swapped(p, "core") for p in planes]


def split3(value):
    high = value.astype(BF)
    rest = value - high.astype(F32)
    middle = rest.astype(BF)
    low = (rest - middle.astype(F32)).astype(BF)
    return high, middle, low


def dot(left, right):
    return jnp.dot(left, right, preferred_element_type=F32)


def row_block(i, rows):
    return pl.ds(pl.multiple_of(i * rows, rows), rows)


def spread_product(cols_ref, rows_ref, operand, sink):
    count = DOFS // CHUNKS

    def step(i, carry):
        part = row_block(i, count)
        key = cols_ref[part, 1:2]
        sign = cols_ref[part, 2:3].astype(F32)
        pick = jnp.where(key == rows_ref[0:1, :], sign, 0.0).astype(BF)
        sink(part, dot(pick, operand[...]))
        return carry

    lax.fori_loop(0, CHUNKS, step, 0)


def slots_product(cols_ref, rows_ref, operand, target):
    count = COUNT * SLAB // CHUNKS

    def step(i, carry):
        part = row_block(i, count)
        key = cols_ref[part, 0:1]
        sign = rows_ref[2:3, 0:DOFS].astype(F32)
        pick = jnp.where(key == rows_ref[1:2, 0:DOFS], sign, 0.0).astype(BF)
        target[part, :] = dot(pick, operand[...]).astype(BF)
        return carry

    lax.fori_loop(0, CHUNKS, step, 0)


def fetch(source, target, sems, i, rows, offset=0):
    part = row_block(i, rows)
    where = pl.ds(pl.multiple_of(offset + i * rows, rows), rows)
    return pltpu.make_async_copy(source.at[where, :], target.at[part, :], sems.at[i])


def column_total(left, right):
    terms = left * right
    return jnp.sum(terms.reshape(terms.shape[0] // 8, 8, -1), axis=0)


def spread_total(total):
    return jnp.broadcast_to(jnp.sum(total, axis=0, keepdims=True), total.shape)


def start_kernel(wanted_ref, jump_ref, *outs):
    high, middle, _ = split3(jump_ref[...])
    rows = jump_ref.shape[0]
    for p in range(COUNT):
        names = wanted_ref[p * SLAB : p * SLAB + CAP, 0:1]
        pick = (lax.broadcasted_iota(jnp.int32, (CAP, rows), 1) + 1 == names).astype(F32).astype(BF)
        outs[p][...] = dot(pick, high) + dot(pick, middle)


def slots_of(p):
    own = slice(p * SLAB, p * SLAB + CAP)
    far = slice(p * SLAB + CAP, (p + 1) * SLAB)
    return own, far


def schur_kernel(first, *refs):
    refs = list(refs)
    take = lambda n: [refs.pop(0) for _ in range(n)]
    own0, far0 = take(COUNT), take(COUNT)
    if not first:
        mine, theirs = take(COUNT), take(COUNT)
        energy_ref, curve_ref = take(2)
    cols_ref, rows_ref, schur_hbm = take(3)
    outs = take(COUNT)
    (energy_out,) = take(1)
    if not first:
        (residual_out,) = take(1)
    schur_v, jump, dofs, product, slot_product, sems = refs
    rows = DOFS // CHUNKS
    for i in range(CHUNKS):
        fetch(schur_hbm, schur_v, sems, i, rows).start()
    if not first:
        step = energy_ref[0:1, :] / curve_ref[0:1, :]
    for p in range(COUNT):
        own, far = slots_of(p)
        own_value = own0[p][...]
        far_value = far0[p][...]
        if not first:
            top, bottom = mine[p][0:CAP, :].astype(F32), mine[p][CAP:SLAB, :].astype(F32)
            own_value = own_value - step * (top + theirs[p][CAP:SLAB, :].astype(F32))
            far_value = far_value - step * (bottom + theirs[p][0:CAP, :].astype(F32))
            residual_out[p * CAP : (p + 1) * CAP, :] = own_value
        jump[own, :] = own_value.astype(BF)
        jump[far, :] = far_value.astype(BF)

    def put(part, result):
        dofs[part, :] = result.astype(BF)

    spread_product(cols_ref, rows_ref, jump, put)

    def step_rows(i, total):
        fetch(schur_hbm, schur_v, sems, i, rows).wait()
        part = row_block(i, rows)
        block = dot(schur_v[part, :], dofs[...]).astype(BF)
        product[part, :] = block
        return total + column_total(dofs[part, :].astype(F32), block.astype(F32))

    total = lax.fori_loop(0, CHUNKS, step_rows, jnp.zeros((8, dofs.shape[1]), F32))
    energy_out[...] = spread_total(total)
    slots_product(cols_ref, rows_ref, product, slot_product)
    for p in range(COUNT):
        outs[p][...] = slot_product[p * SLAB : (p + 1) * SLAB, :]


def jump_kernel(wide, *refs):
    refs = list(refs)
    take = lambda n: [refs.pop(0) for _ in range(n)]
    mine, theirs = take(COUNT), take(COUNT)
    energy_ref, coupling_ref = take(2)
    if wide:
        (names_ref,) = take(1)
    cols_ref, rows_ref = take(2)
    dofs_out, coarse_out, direction_out = take(3)
    (jump,) = refs
    for p in range(COUNT):
        own, far = slots_of(p)
        top, bottom = mine[p][0:CAP, :].astype(F32), mine[p][CAP:SLAB, :].astype(F32)
        own_value = top + theirs[p][CAP:SLAB, :].astype(F32)
        far_value = bottom + theirs[p][0:CAP, :].astype(F32)
        direction_out[p * CAP : (p + 1) * CAP, :] = own_value
        jump[own, :] = own_value.astype(BF)
        jump[far, :] = far_value.astype(BF)

    def put(part, result):
        dofs_out[part, :] = result.astype(BF)

    spread_product(cols_ref, rows_ref, jump, put)
    corner = dot(coupling_ref[...], dofs_out[...])
    energy = energy_ref[0:1, :]
    high, middle, low = split3(energy)
    extra = jnp.concatenate(
        [high.astype(F32), middle.astype(F32), low.astype(F32), jnp.zeros((5, energy.shape[1]), F32)],
        axis=0,
    )
    rows = jnp.concatenate([corner, extra], axis=0)
    if wide:
        rows = jnp.concatenate([rows, names_ref[...]], axis=1)
    coarse_out[...] = rows.astype(BF)


def local_kernel(half, dofs_ref, inverse_hbm, out, inverse_v, sems):
    count = out.shape[0]
    rows = count // CHUNKS
    offset = half * count
    copy = lambda i: fetch(inverse_hbm, inverse_v, sems, i, rows, offset)
    for i in range(2):
        copy(i).start()

    def step(i, carry):
        copy(i).wait()

        @pl.when(i + 2 < CHUNKS)
        def _():
            copy(i + 2).start()

        part = row_block(i, rows)
        out[part, :] = dot(inverse_v[part, :], dofs_ref[...])
        return carry

    lax.fori_loop(0, CHUNKS, step, 0)


def coarse_kernel(first, *refs):
    refs = list(refs)
    take = lambda n: [refs.pop(0) for _ in range(n)]
    pieces = take(8)
    (table_ref,) = take(1)
    outs = take(4)
    columns = outs[0].shape[1]
    if first:
        (select_out,) = refs
        high, middle, low = split3(table_ref[...])
        size = table_ref.shape[1]
        contract = (((1,), (1,)), ((), ()))
        names = jnp.concatenate([ref[:, columns : columns + 128] for ref in pieces], axis=0)
        names = names.astype(F32)
        index = (names[:, 0:1] * 32.0 + names[:, 1:2]).astype(jnp.int32)
        pick = lax.broadcasted_iota(jnp.int32, (names.shape[0], size), 1) == index
        pick = pick.astype(F32).astype(BF)
        select = sum(
            lax.dot_general(piece, pick, contract, preferred_element_type=F32)
            for piece in (high, middle, low)
        )
        row = lax.broadcasted_iota(jnp.int32, select.shape, 0) % 32
        lane = lax.broadcasted_iota(jnp.int32, select.shape, 1) % 32
        energy = (lane >= 24) & (lane < 27)
        select = jnp.where(row < 24, select, jnp.where((row == 24) & energy, 1.0, 0.0))
        select_out[...] = select
    else:
        select = table_ref[...]
    block = jnp.concatenate([ref[:, 0:columns] for ref in pieces], axis=0)
    total = None
    for piece in split3(select):
        term = dot(piece, block)
        total = term if total is None else total + term
    for i in range(4):
        outs[i][...] = total[32 * i : 32 * i + 32, :]


def flex_kernel(first, *refs):
    refs = list(refs)
    take = lambda n: [refs.pop(0) for _ in range(n)]
    parts = take(4)
    local_refs = take(2)
    coupling_ref, dofs_ref = take(2)
    if not first:
        before_ref, energy_ref, old_dofs_ref = take(3)
    cols_ref, rows_ref = take(2)
    outs = take(COUNT)
    if not first:
        keeps = take(COUNT)
    energy_out, curve_out = take(2)
    if first:
        (before_out,) = take(1)
    product, slot_product = refs
    coarse = parts[0][...] + parts[1][...] + parts[2][...] + parts[3][...]
    energy_out[...] = jnp.broadcast_to(coarse[24:25, :], energy_out.shape)
    solution_rows = coarse[0:24, :].astype(BF)
    ratio = None if first else coarse[24:25, :] / energy_ref[0:1, :]
    half = DOFS // 2
    total = jnp.zeros(curve_out.shape, F32)
    for i in range(2):
        part = slice(i * half, (i + 1) * half)
        back = lax.dot_general(
            coupling_ref[:, part],
            solution_rows,
            (((0,), (0,)), ((), ())),
            preferred_element_type=F32,
        )
        whole = local_refs[i][...] + back
        direction = dofs_ref[part, :].astype(F32)
        if first:
            before_out[part, :] = whole
        else:
            whole = whole + ratio * before_ref[part, :]
            direction = direction + ratio * old_dofs_ref[part, :].astype(F32)
        block = whole.astype(BF)
        product[part, :] = block
        total = total + column_total(direction, block.astype(F32))
    curve_out[...] = spread_total(total)
    slots_product(cols_ref, rows_ref, product, slot_product)
    for p in range(COUNT):
        own, far = slots_of(p)
        if first:
            outs[p][...] = slot_product[p * SLAB : (p + 1) * SLAB, :]
        else:
            keeps[p][...] = slot_product[own, :]
            outs[p][...] = slot_product[far, :]


def final_kernel(*refs):
    refs = list(refs)
    take = lambda n: [refs.pop(0) for _ in range(n)]
    keeps, gots = take(COUNT), take(COUNT)
    residual_ref, old_ref, new_ref, wanted_ref = take(4)
    e0, c0, e1, c1 = [ref[0:1, :] for ref in take(4)]
    multipliers_out, residual_out = take(2)
    owned = multipliers_out.shape[0]
    step0 = e0 / c0
    step1 = e1 / c1
    ratio = e1 / e0
    old = old_ref[...]
    xs = step0 * old + step1 * (new_ref[...] + ratio * old)
    rs = []
    for p in range(COUNT):
        image = keeps[p][...].astype(F32) + gots[p][...].astype(F32)
        rs.append(residual_ref[p * CAP : (p + 1) * CAP, :] - step1 * image)
    names = wanted_ref[...]
    pick = lax.broadcasted_iota(jnp.int32, (owned, names.shape[1]), 0) + 1 == names
    pick = pick.astype(F32).astype(BF)
    for values, out in ((xs, multipliers_out), (jnp.concatenate(rs, axis=0), residual_out)):
        high, middle, _ = split3(values)
        out[...] = dot(pick, high) + dot(pick, middle)


VM = pl.BlockSpec(memory_space=pltpu.VMEM)
HBM = pl.BlockSpec(memory_space=pl.ANY)


def call(kernel, inputs, in_hbm, outs, scratch, flops):
    specs = [VM] * len(inputs) + [HBM] * len(in_hbm)
    moved = sum(x.size * x.dtype.itemsize for x in list(inputs) + list(in_hbm))
    return pl.pallas_call(
        kernel,
        out_shape=[jax.ShapeDtypeStruct(s, d) for s, d in outs],
        in_specs=specs,
        out_specs=[VM] * len(outs),
        scratch_shapes=scratch,
        compiler_params=pltpu.CompilerParams(vmem_limit_bytes=VMEM_LIMIT),
        cost_estimate=pl.CostEstimate(flops=flops, bytes_accessed=moved, transcendentals=0),
    )(*inputs, *in_hbm)


def routing(targets, signs, corners, owned):
    subs = lax.axis_size("sub")
    a = lax.axis_index("sub")
    b = lax.axis_index("nar")
    me = a * NAR + b
    count = targets.shape[0]
    holder = targets // owned
    row = targets - holder * owned
    linked = signs != 0
    home = linked & (holder == me)
    remote = linked & (holder != me)
    kind = (holder // NAR - a + 1) % subs * NAR + (holder % NAR - b) % NAR
    peer = jnp.where(remote, kind - (kind > NAR), COUNT)
    blocks = count // 128
    lanes = peer.reshape(blocks, 128).T
    member = lanes[:, :, None] == jnp.arange(16)[None, None, :]
    member = member.astype(F32).reshape(128, blocks * 16)
    before = jnp.arange(128)[:, None] > jnp.arange(128)[None, :]
    within = dot(before.astype(BF), member.astype(BF)).reshape(128, blocks, 16)
    totals = jnp.sum(member, axis=0).reshape(blocks, 16)
    ahead = jnp.arange(blocks)[:, None] > jnp.arange(blocks)[None, :]
    base = jnp.sum(ahead.astype(F32)[:, :, None] * totals[None, :, :], axis=1)
    rank = jnp.sum(member.reshape(128, blocks, 16) * (within + base[None, :, :]), axis=2)
    rank = rank.T.reshape(count).astype(jnp.int32)
    place = peer * CAP + rank
    far_names = jnp.arange(COUNT * CAP)
    hit = jnp.where(remote, place, -1)[:, None] == far_names[None, :]
    request = jnp.max(jnp.where(hit, (row + 1)[:, None], 0), axis=0).reshape(COUNT, CAP)
    message = jnp.concatenate(
        [
            request,
            jnp.broadcast_to(corners[None, :], (COUNT, corners.shape[0])),
            jnp.zeros((COUNT, 128 - CAP - corners.shape[0]), jnp.int32),
        ],
        axis=1,
    )
    got = jnp.concatenate(routed_exchange([message[p : p + 1, :] for p in range(COUNT)]), axis=0)
    wanted = got[:, :CAP]
    dof_key = jnp.where(home, row + 1, jnp.where(remote, FAR_KEY + place, -2))
    slot_key = jnp.concatenate(
        [jnp.where(wanted > 0, wanted, -1), FAR_KEY + far_names.reshape(COUNT, CAP)], axis=1
    ).reshape(COUNT * SLAB)
    pad = (0, COUNT * SLAB - count)
    keys = [slot_key, jnp.pad(dof_key, pad, constant_values=-3), jnp.pad(signs, pad)]
    mates = [corners] + [
        got[PEERS.index((0, db)), CAP : CAP + corners.shape[0]] for db in range(1, NAR)
    ]
    mates = jnp.concatenate(
        [jnp.pad(names, (0, 32 - names.shape[0])) for names in mates], axis=0
    )
    return wanted.reshape(1, COUNT * CAP), jnp.stack(keys, axis=1), jnp.stack(keys, axis=0), mates


def solve(
    remainder_inverse,
    dirichlet_schur,
    corner_coupling,
    coarse_inverse,
    jump_load,
    dof_multiplier,
    dof_sign,
    corner_index,
):
    inverse = remainder_inverse[0]
    schur = dirichlet_schur[0]
    coupling = corner_coupling[0]
    corners = corner_index[0]
    owned, columns = jump_load.shape
    wanted, cols, rows, mates = routing(dof_multiplier[0], dof_sign[0], corners, owned)
    coarse_rows = coarse_inverse[mates]
    names = jnp.pad(corners, (0, 32 - corners.shape[0]), constant_values=1023)
    names = jnp.stack([names // 32, names % 32], axis=1).astype(F32)
    names = jnp.pad(names, ((0, 0), (0, 126)))

    slots_n = COUNT * SLAB
    small = ((8, columns), F32)
    slab_outs = [((SLAB, columns), BF)] * COUNT
    half_outs = [((CAP, columns), BF)] * COUNT
    own_out = ((COUNT * CAP, columns), F32)
    square_v = pltpu.VMEM((DOFS, DOFS), BF)
    half_v = pltpu.VMEM((DOFS // 2, DOFS), BF)
    slot_b = pltpu.VMEM((slots_n, columns), BF)
    dof_b = pltpu.VMEM((DOFS, columns), BF)
    sems = pltpu.SemaphoreType.DMA((CHUNKS,))
    one = 2 * DOFS * slots_n * columns

    own0 = call(
        start_kernel,
        [cols, jump_load],
        [],
        [((CAP, columns), F32)] * COUNT,
        [],
        4 * COUNT * CAP * owned * columns,
    )
    far0 = exchange(own0)

    def precondition(first, extra):
        return call(
            functools.partial(schur_kernel, first),
            [*own0, *far0, *extra, cols, rows],
            [schur],
            slab_outs + [small] + ([] if first else [own_out]),
            [square_v, slot_b, dof_b, dof_b, slot_b, sems],
            3 * one,
        )

    def jumped(mine, theirs, energy, wide):
        return call(
            functools.partial(jump_kernel, wide),
            [*mine, *theirs, energy, coupling] + ([names] if wide else []) + [cols, rows],
            [],
            [
                ((DOFS, columns), BF),
                ((32, columns + (128 if wide else 0)), BF),
                own_out,
            ],
            [slot_b],
            one,
        )

    def local(dofs, half):
        return call(
            functools.partial(local_kernel, half),
            [dofs],
            [inverse],
            [((DOFS // 2, columns), F32)],
            [half_v, sems],
            one // 2,
        )[0]

    def coarse(part, dofs, table, first):
        low = local(dofs, 0)
        pieces = line_gather(part, low)
        parts = call(
            functools.partial(coarse_kernel, first),
            [*pieces, table],
            [],
            [((32, columns), F32)] * 4 + ([((128, 1024), F32)] if first else []),
            [],
            10**9,
        )
        sums = [parts[0]] + [shifted(parts[k], "y", k) for k in (1, 3, 2)]
        high = local(dofs, 1)
        return [*sums, low, high], parts[4:]

    *reduced, energy_part = precondition(True, [])
    reduced_got = exchange(reduced)
    dofs, coarse_part, direction = jumped(reduced, reduced_got, energy_part, True)
    parts, (select,) = coarse(coarse_part, dofs, coarse_rows, True)
    *image, energy0, curve_part, before = call(
        functools.partial(flex_kernel, True),
        [*parts, coupling, dofs, cols, rows],
        [],
        slab_outs + [small, small, ((DOFS, columns), F32)],
        [dof_b, slot_b],
        one,
    )
    image_got, curve0 = exchange_and_sum(image, curve_part)

    *reduced, energy_part, residual1 = precondition(False, [*image, *image_got, energy0, curve0])
    reduced_got = exchange(reduced)
    dofs1, coarse_part, direction1 = jumped(reduced, reduced_got, energy_part, False)
    parts, _ = coarse(coarse_part, dofs1, select, False)
    flexed = call(
        functools.partial(flex_kernel, False),
        [*parts, coupling, dofs1, before, energy0, dofs, cols, rows],
        [],
        half_outs + half_outs + [small, small],
        [dof_b, slot_b],
        one,
    )
    sent, kept = flexed[:COUNT], flexed[COUNT : 2 * COUNT]
    energy1, curve_part = flexed[2 * COUNT :]
    got, curve1 = exchange_and_sum(sent, curve_part)
    return tuple(
        call(
            final_kernel,
            [*kept, *got, residual1, direction, direction1, wanted]
            + [energy0, curve0, energy1, curve1],
            [],
            [((owned, columns), F32)] * 2,
            [],
            8 * COUNT * CAP * owned * columns,
        )
    )


def solution(mesh):
    placed = (
        P(AXES, None, None),
        P(AXES, None, None),
        P(AXES, None, None),
        P(),
        P(AXES, None),
        P(AXES, None),
        P(AXES, None),
        P(AXES, None),
    )
    return jax.shard_map(
        solve,
        mesh=mesh,
        in_specs=placed,
        out_specs=(P(AXES, None), P(AXES, None)),
        check_vma=False,
    )
```

```python
import functools

import jax
import jax.numpy as jnp
from jax import lax
from jax.experimental import pallas as pl
from jax.experimental.pallas import tpu as pltpu
from jax.sharding import PartitionSpec as P


CAP = 96
SLAB = 2 * CAP
NAR = 4
AXES = ("sub", "nar")
PEERS = [(side, db) for side in (0, 1, 2) for db in range(NAR) if (side, db) != (0, 0)]
COUNT = len(PEERS)
ORDER = [PEERS.index((side, db)) for db in (1, 3, 2, 0) for side in (2, 0, 1) if (side, db) != (0, 0)]
FAR_KEY = 1000
CHUNKS = 4
DOFS = 2048
BF = jnp.bfloat16
F32 = jnp.float32


def mirror(p):
    side, db = PEERS[p]
    return PEERS.index((side, -db % NAR))


def beside(a, side, subs):
    if side == 0:
        return a
    return a ^ 1 if side == 1 else (a + 1 if a % 2 else a - 1) % subs


def peer_pairs(p, subs):
    side, db = PEERS[p]
    return [
        (a * NAR + b, beside(a, side, subs) * NAR + (b + db) % NAR)
        for a in range(subs)
        for b in range(NAR)
    ]


def swap_pairs(kind, subs):
    def other(a, b):
        z, x, core = a // 8, a // 2 % 4, a % 2
        if kind == "core":
            core ^= 1
        elif kind == "x1":
            x ^= 1
        elif kind == "x3":
            x = 3 - x
        elif kind == "z1":
            z ^= 1
        elif kind == "z3":
            z = 3 - z
        elif kind == "y1":
            b ^= 1
        elif kind == "y3":
            b = 3 - b
        return (z * 8 + x * 2 + core) * NAR + b

    return [(a * NAR + b, other(a, b)) for a in range(subs) for b in range(NAR)]


def exchange(slabs):
    subs = lax.axis_size("sub")
    got = [None] * COUNT
    for p in ORDER:
        got[mirror(p)] = lax.ppermute(slabs[p], AXES, peer_pairs(p, subs))
    return got


def shifted(block, axis, by):
    subs = lax.axis_size("sub")

    def other(a, b):
        z, x, core = a // 8, a // 2 % 4, a % 2
        if axis == "z":
            z = (z + by) % 4
        elif axis == "x":
            x = (x + by) % 4
        else:
            b = (b + by) % NAR
        return (z * 8 + x * 2 + core) * NAR + b

    pairs = [(a * NAR + b, other(a, b)) for a in range(subs) for b in range(NAR)]
    return lax.ppermute(block, AXES, pairs)


def swapped(block, kind):
    return lax.ppermute(block, AXES, swap_pairs(kind, lax.axis_size("sub")))


def after(block, gate):
    return lax.optimization_barrier((block, gate))[0]


SUM_KINDS = ("core", "y1", "y3", "x1", "x3", "z1", "z3")


def exchange_and_sum(slabs, block):
    subs = lax.axis_size("sub")
    got = [None] * COUNT
    for p in ORDER:
        got[mirror(p)] = lax.ppermute(slabs[p], AXES, peer_pairs(p, subs))
    for kind in SUM_KINDS:
        arrived = swapped(block, kind)
        block = block + arrived
    return got, block


def routed_exchange(messages):
    subs = lax.axis_size("sub")
    index = PEERS.index
    one = lambda side: [
        (a * NAR + b, beside(a, side, subs) * NAR + b) for a in range(subs) for b in range(NAR)
    ]
    bundle = lambda side: jnp.concatenate([messages[index((side, db))] for db in range(NAR)], axis=0)
    near = lax.ppermute(bundle(1), AXES, one(1))
    far = lax.ppermute(bundle(2), AXES, one(2))
    got = [None] * COUNT
    got[index((1, 0))] = near[0:1]
    got[index((2, 0))] = far[0:1]
    for db in (1, 3, 2):
        pack = jnp.concatenate(
            [messages[index((0, db))], near[db : db + 1], far[db : db + 1]], axis=0
        )
        arrived = shifted(pack, "y", db)
        back = -db % NAR
        for side in range(3):
            got[index((side, back))] = arrived[side : side + 1]
    return got


def line_gather(block, gate):
    rows = [block] + [shifted(block, "x", k) for k in (1, 3, 2)]
    plane = jnp.concatenate(rows, axis=0)
    planes = [plane] + [shifted(plane, "z", k) for k in (1, 3, 2)]
    planes[3] = after(planes[3], gate)
    return planes + [swapped(p, "core") for p in planes]


def split3(value):
    high = value.astype(BF)
    rest = value - high.astype(F32)
    middle = rest.astype(BF)
    low = (rest - middle.astype(F32)).astype(BF)
    return high, middle, low


def dot(left, right):
    return jnp.dot(left, right, preferred_element_type=F32)


def row_block(i, rows):
    return pl.ds(pl.multiple_of(i * rows, rows), rows)


def spread_product(cols_ref, rows_ref, operand, sink):
    count = DOFS // CHUNKS

    def step(i, carry):
        part = row_block(i, count)
        key = cols_ref[part, 1:2]
        sign = cols_ref[part, 2:3].astype(F32)
        pick = jnp.where(key == rows_ref[0:1, :], sign, 0.0).astype(BF)
        sink(part, dot(pick, operand[...]))
        return carry

    lax.fori_loop(0, CHUNKS, step, 0)


def slots_product(cols_ref, rows_ref, operand, target):
    count = COUNT * SLAB // CHUNKS

    def step(i, carry):
        part = row_block(i, count)
        key = cols_ref[part, 0:1]
        sign = rows_ref[2:3, 0:DOFS].astype(F32)
        pick = jnp.where(key == rows_ref[1:2, 0:DOFS], sign, 0.0).astype(BF)
        target[part, :] = dot(pick, operand[...]).astype(BF)
        return carry

    lax.fori_loop(0, CHUNKS, step, 0)


def column_total(left, right):
    terms = left * right
    return jnp.sum(terms.reshape(terms.shape[0] // 8, 8, -1), axis=0)


def spread_total(total):
    return jnp.broadcast_to(jnp.sum(total, axis=0, keepdims=True), total.shape)


def start_kernel(wanted_ref, jump_ref, *outs):
    high, middle, _ = split3(jump_ref[...])
    rows = jump_ref.shape[0]
    for p in range(COUNT):
        names = wanted_ref[p * SLAB : p * SLAB + CAP, 0:1]
        pick = (lax.broadcasted_iota(jnp.int32, (CAP, rows), 1) + 1 == names).astype(F32).astype(BF)
        outs[p][...] = dot(pick, high) + dot(pick, middle)


def slots_of(p):
    own = slice(p * SLAB, p * SLAB + CAP)
    far = slice(p * SLAB + CAP, (p + 1) * SLAB)
    return own, far


def schur_kernel(first, *refs):
    refs = list(refs)
    take = lambda n: [refs.pop(0) for _ in range(n)]
    own0, far0 = take(COUNT), take(COUNT)
    if not first:
        mine, theirs = take(COUNT), take(COUNT)
        energy_ref, curve_ref = take(2)
    cols_ref, rows_ref, schur_v = take(3)
    outs = take(COUNT)
    (energy_out,) = take(1)
    if not first:
        (residual_out,) = take(1)
    jump, dofs, product, slot_product = refs
    rows = DOFS // CHUNKS
    if not first:
        step = energy_ref[0:1, :] / curve_ref[0:1, :]
    for p in range(COUNT):
        own, far = slots_of(p)
        own_value = own0[p][...]
        far_value = far0[p][...]
        if not first:
            top, bottom = mine[p][0:CAP, :].astype(F32), mine[p][CAP:SLAB, :].astype(F32)
            own_value = own_value - step * (top + theirs[p][CAP:SLAB, :].astype(F32))
            far_value = far_value - step * (bottom + theirs[p][0:CAP, :].astype(F32))
            residual_out[p * CAP : (p + 1) * CAP, :] = own_value
        jump[own, :] = own_value.astype(BF)
        jump[far, :] = far_value.astype(BF)

    def put(part, result):
        dofs[part, :] = result.astype(BF)

    spread_product(cols_ref, rows_ref, jump, put)

    def step_rows(i, total):
        part = row_block(i, rows)
        block = dot(schur_v[part, :], dofs[...]).astype(BF)
        product[part, :] = block
        return total + column_total(dofs[part, :].astype(F32), block.astype(F32))

    total = lax.fori_loop(0, CHUNKS, step_rows, jnp.zeros((8, dofs.shape[1]), F32))
    energy_out[...] = spread_total(total)
    slots_product(cols_ref, rows_ref, product, slot_product)
    for p in range(COUNT):
        outs[p][...] = slot_product[p * SLAB : (p + 1) * SLAB, :]


def jump_kernel(wide, *refs):
    refs = list(refs)
    take = lambda n: [refs.pop(0) for _ in range(n)]
    mine, theirs = take(COUNT), take(COUNT)
    energy_ref, coupling_ref = take(2)
    if wide:
        (names_ref,) = take(1)
    cols_ref, rows_ref = take(2)
    dofs_out, coarse_out, direction_out = take(3)
    (jump,) = refs
    for p in range(COUNT):
        own, far = slots_of(p)
        top, bottom = mine[p][0:CAP, :].astype(F32), mine[p][CAP:SLAB, :].astype(F32)
        own_value = top + theirs[p][CAP:SLAB, :].astype(F32)
        far_value = bottom + theirs[p][0:CAP, :].astype(F32)
        direction_out[p * CAP : (p + 1) * CAP, :] = own_value
        jump[own, :] = own_value.astype(BF)
        jump[far, :] = far_value.astype(BF)

    def put(part, result):
        dofs_out[part, :] = result.astype(BF)

    spread_product(cols_ref, rows_ref, jump, put)
    corner = dot(coupling_ref[...], dofs_out[...])
    energy = energy_ref[0:1, :]
    high, middle, low = split3(energy)
    extra = jnp.concatenate(
        [high.astype(F32), middle.astype(F32), low.astype(F32), jnp.zeros((5, energy.shape[1]), F32)],
        axis=0,
    )
    rows = jnp.concatenate([corner, extra], axis=0)
    if wide:
        rows = jnp.concatenate([rows, names_ref[...]], axis=1)
    coarse_out[...] = rows.astype(BF)


def local_kernel(half, dofs_ref, inverse_ref, out):
    rows = DOFS // CHUNKS
    count = out.shape[0]

    def step(i, carry):
        part = pl.ds(pl.multiple_of(half * count + i * rows, rows), rows)
        out[row_block(i, rows), :] = dot(inverse_ref[part, :], dofs_ref[...])
        return carry

    lax.fori_loop(0, count // rows, step, 0)


def coarse_kernel(first, *refs):
    refs = list(refs)
    take = lambda n: [refs.pop(0) for _ in range(n)]
    pieces = take(8)
    (table_ref,) = take(1)
    outs = take(4)
    columns = outs[0].shape[1]
    if first:
        (select_out,) = refs
        high, middle, low = split3(table_ref[...])
        size = table_ref.shape[1]
        contract = (((1,), (1,)), ((), ()))
        names = jnp.concatenate([ref[:, columns : columns + 128] for ref in pieces], axis=0)
        names = names.astype(F32)
        index = (names[:, 0:1] * 32.0 + names[:, 1:2]).astype(jnp.int32)
        pick = lax.broadcasted_iota(jnp.int32, (names.shape[0], size), 1) == index
        pick = pick.astype(F32).astype(BF)
        select = sum(
            lax.dot_general(piece, pick, contract, preferred_element_type=F32)
            for piece in (high, middle, low)
        )
        row = lax.broadcasted_iota(jnp.int32, select.shape, 0) % 32
        lane = lax.broadcasted_iota(jnp.int32, select.shape, 1) % 32
        energy = (lane >= 24) & (lane < 27)
        select = jnp.where(row < 24, select, jnp.where((row == 24) & energy, 1.0, 0.0))
        select_out[...] = select
    else:
        select = table_ref[...]
    block = jnp.concatenate([ref[:, 0:columns] for ref in pieces], axis=0)
    total = None
    for piece in split3(select):
        term = dot(piece, block)
        total = term if total is None else total + term
    for i in range(4):
        outs[i][...] = total[32 * i : 32 * i + 32, :]


def flex_kernel(first, *refs):
    refs = list(refs)
    take = lambda n: [refs.pop(0) for _ in range(n)]
    parts = take(4)
    local_refs = take(2)
    coupling_ref, dofs_ref = take(2)
    if not first:
        before_ref, energy_ref, old_dofs_ref = take(3)
    cols_ref, rows_ref = take(2)
    outs = take(COUNT)
    if not first:
        keeps = take(COUNT)
    energy_out, curve_out = take(2)
    if first:
        (before_out,) = take(1)
    product, slot_product = refs
    coarse = parts[0][...] + parts[1][...] + parts[2][...] + parts[3][...]
    energy_out[...] = jnp.broadcast_to(coarse[24:25, :], energy_out.shape)
    solution_rows = coarse[0:24, :].astype(BF)
    ratio = None if first else coarse[24:25, :] / energy_ref[0:1, :]
    half = DOFS // 2
    total = jnp.zeros(curve_out.shape, F32)
    for i in range(2):
        part = slice(i * half, (i + 1) * half)
        back = lax.dot_general(
            coupling_ref[:, part],
            solution_rows,
            (((0,), (0,)), ((), ())),
            preferred_element_type=F32,
        )
        whole = local_refs[i][...] + back
        direction = dofs_ref[part, :].astype(F32)
        if first:
            before_out[part, :] = whole
        else:
            whole = whole + ratio * before_ref[part, :]
            direction = direction + ratio * old_dofs_ref[part, :].astype(F32)
        block = whole.astype(BF)
        product[part, :] = block
        total = total + column_total(direction, block.astype(F32))
    curve_out[...] = spread_total(total)
    slots_product(cols_ref, rows_ref, product, slot_product)
    for p in range(COUNT):
        own, far = slots_of(p)
        if first:
            outs[p][...] = slot_product[p * SLAB : (p + 1) * SLAB, :]
        else:
            keeps[p][...] = slot_product[own, :]
            outs[p][...] = slot_product[far, :]


def final_kernel(*refs):
    refs = list(refs)
    take = lambda n: [refs.pop(0) for _ in range(n)]
    keeps, gots = take(COUNT), take(COUNT)
    residual_ref, old_ref, new_ref, wanted_ref = take(4)
    e0, c0, e1, c1 = [ref[0:1, :] for ref in take(4)]
    multipliers_out, residual_out = take(2)
    owned = multipliers_out.shape[0]
    step0 = e0 / c0
    step1 = e1 / c1
    ratio = e1 / e0
    old = old_ref[...]
    xs = step0 * old + step1 * (new_ref[...] + ratio * old)
    rs = []
    for p in range(COUNT):
        image = keeps[p][...].astype(F32) + gots[p][...].astype(F32)
        rs.append(residual_ref[p * CAP : (p + 1) * CAP, :] - step1 * image)
    names = wanted_ref[...]
    pick = lax.broadcasted_iota(jnp.int32, (owned, names.shape[1]), 0) + 1 == names
    pick = pick.astype(F32).astype(BF)
    for values, out in ((xs, multipliers_out), (jnp.concatenate(rs, axis=0), residual_out)):
        high, middle, _ = split3(values)
        out[...] = dot(pick, high) + dot(pick, middle)


VM = pl.BlockSpec(memory_space=pltpu.VMEM)


def call(kernel, inputs, outs, scratch, flops, grant=24):
    moved = sum(x.size * x.dtype.itemsize for x in inputs)
    return pl.pallas_call(
        kernel,
        out_shape=[jax.ShapeDtypeStruct(s, d) for s, d in outs],
        in_specs=[VM] * len(inputs),
        out_specs=[VM] * len(outs),
        scratch_shapes=scratch,
        compiler_params=pltpu.CompilerParams(vmem_limit_bytes=grant * 1024 * 1024),
        cost_estimate=pl.CostEstimate(flops=flops, bytes_accessed=moved, transcendentals=0),
    )(*inputs)


def routing(targets, signs, corners, owned):
    subs = lax.axis_size("sub")
    a = lax.axis_index("sub")
    b = lax.axis_index("nar")
    me = a * NAR + b
    count = targets.shape[0]
    holder = targets // owned
    row = targets - holder * owned
    linked = signs != 0
    home = linked & (holder == me)
    remote = linked & (holder != me)
    turn = jnp.where(a % 2 == 0, 1, -1)
    step = (holder // NAR - a) % subs
    side = jnp.where(step == 0, 0, jnp.where(step == turn % subs, 1, 2))
    peer = jnp.where(remote, side * NAR + (holder % NAR - b) % NAR - 1, COUNT)
    blocks = count // 128
    lanes = peer.reshape(blocks, 128).T
    member = lanes[:, :, None] == jnp.arange(16)[None, None, :]
    member = member.astype(F32).reshape(128, blocks * 16)
    before = jnp.arange(128)[:, None] > jnp.arange(128)[None, :]
    within = dot(before.astype(BF), member.astype(BF)).reshape(128, blocks, 16)
    totals = jnp.sum(member, axis=0).reshape(blocks, 16)
    ahead = jnp.arange(blocks)[:, None] > jnp.arange(blocks)[None, :]
    base = jnp.sum(ahead.astype(F32)[:, :, None] * totals[None, :, :], axis=1)
    rank = jnp.sum(member.reshape(128, blocks, 16) * (within + base[None, :, :]), axis=2)
    rank = rank.T.reshape(count).astype(jnp.int32)
    place = peer * CAP + rank
    far_names = jnp.arange(COUNT * CAP)
    hit = jnp.where(remote, place, -1)[:, None] == far_names[None, :]
    request = jnp.max(jnp.where(hit, (row + 1)[:, None], 0), axis=0).reshape(COUNT, CAP)
    message = jnp.concatenate(
        [
            request,
            jnp.broadcast_to(corners[None, :], (COUNT, corners.shape[0])),
            jnp.zeros((COUNT, 128 - CAP - corners.shape[0]), jnp.int32),
        ],
        axis=1,
    )
    got = jnp.concatenate(routed_exchange([message[p : p + 1, :] for p in range(COUNT)]), axis=0)
    wanted = got[:, :CAP]
    dof_key = jnp.where(home, row + 1, jnp.where(remote, FAR_KEY + place, -2))
    slot_key = jnp.concatenate(
        [jnp.where(wanted > 0, wanted, -1), FAR_KEY + far_names.reshape(COUNT, CAP)], axis=1
    ).reshape(COUNT * SLAB)
    pad = (0, COUNT * SLAB - count)
    keys = [slot_key, jnp.pad(dof_key, pad, constant_values=-3), jnp.pad(signs, pad)]
    mates = [corners] + [
        got[PEERS.index((0, db)), CAP : CAP + corners.shape[0]] for db in range(1, NAR)
    ]
    mates = jnp.concatenate(
        [jnp.pad(names, (0, 32 - names.shape[0])) for names in mates], axis=0
    )
    return wanted.reshape(1, COUNT * CAP), jnp.stack(keys, axis=1), jnp.stack(keys, axis=0), mates


def solve(
    remainder_inverse,
    dirichlet_schur,
    corner_coupling,
    coarse_inverse,
    jump_load,
    dof_multiplier,
    dof_sign,
    corner_index,
):
    inverse = remainder_inverse[0]
    schur = dirichlet_schur[0]
    coupling = corner_coupling[0]
    corners = corner_index[0]
    owned, columns = jump_load.shape
    wanted, cols, rows, mates = routing(dof_multiplier[0], dof_sign[0], corners, owned)
    coarse_rows = coarse_inverse[mates]
    names = jnp.pad(corners, (0, 32 - corners.shape[0]), constant_values=1023)
    names = jnp.stack([names // 32, names % 32], axis=1).astype(F32)
    names = jnp.pad(names, ((0, 0), (0, 126)))

    slots_n = COUNT * SLAB
    small = ((8, columns), F32)
    slab_outs = [((SLAB, columns), BF)] * COUNT
    half_outs = [((CAP, columns), BF)] * COUNT
    own_out = ((COUNT * CAP, columns), F32)
    slot_b = pltpu.VMEM((slots_n, columns), BF)
    dof_b = pltpu.VMEM((DOFS, columns), BF)
    one = 2 * DOFS * slots_n * columns

    own0 = call(
        start_kernel,
        [cols, jump_load],
        [((CAP, columns), F32)] * COUNT,
        [],
        4 * COUNT * CAP * owned * columns,
    )
    far0 = exchange(own0)

    def precondition(first, extra):
        return call(
            functools.partial(schur_kernel, first),
            [*own0, *far0, *extra, cols, rows, schur],
            slab_outs + [small] + ([] if first else [own_out]),
            [slot_b, dof_b, dof_b, slot_b],
            3 * one,
        )

    def jumped(mine, theirs, energy, wide):
        return call(
            functools.partial(jump_kernel, wide),
            [*mine, *theirs, energy, coupling] + ([names] if wide else []) + [cols, rows],
            [
                ((DOFS, columns), BF),
                ((32, columns + (128 if wide else 0)), BF),
                own_out,
            ],
            [slot_b],
            one,
        )

    def local(dofs, half):
        return call(
            functools.partial(local_kernel, half),
            [dofs, inverse],
            [((DOFS // 2, columns), F32)],
            [],
            one // 2,
        )[0]

    def coarse(part, dofs, table, first):
        low = local(dofs, 0)
        pieces = line_gather(part, low)
        parts = call(
            functools.partial(coarse_kernel, first),
            [*pieces, table],
            [((32, columns), F32)] * 4 + ([((128, 1024), F32)] if first else []),
            [],
            10**9,
        )
        sums = [parts[0]] + [shifted(parts[k], "y", k) for k in (1, 3, 2)]
        high = local(dofs, 1)
        return [*sums, low, high], parts[4:]

    *reduced, energy_part = precondition(True, [])
    reduced_got = exchange(reduced)
    dofs, coarse_part, direction = jumped(reduced, reduced_got, energy_part, True)
    parts, (select,) = coarse(coarse_part, dofs, coarse_rows, True)
    *image, energy0, curve_part, before = call(
        functools.partial(flex_kernel, True),
        [*parts, coupling, dofs, cols, rows],
        slab_outs + [small, small, ((DOFS, columns), F32)],
        [dof_b, slot_b],
        one,
    )
    image_got, curve0 = exchange_and_sum(image, curve_part)

    *reduced, energy_part, residual1 = precondition(False, [*image, *image_got, energy0, curve0])
    reduced_got = exchange(reduced)
    dofs1, coarse_part, direction1 = jumped(reduced, reduced_got, energy_part, False)
    parts, _ = coarse(coarse_part, dofs1, select, False)
    flexed = call(
        functools.partial(flex_kernel, False),
        [*parts, coupling, dofs1, before, energy0, dofs, cols, rows],
        half_outs + half_outs + [small, small],
        [dof_b, slot_b],
        one,
    )
    sent, kept = flexed[:COUNT], flexed[COUNT : 2 * COUNT]
    energy1, curve_part = flexed[2 * COUNT :]
    got, curve1 = exchange_and_sum(sent, curve_part)
    return tuple(
        call(
            final_kernel,
            [*kept, *got, residual1, direction, direction1, wanted]
            + [energy0, curve0, energy1, curve1],
            [((owned, columns), F32)] * 2,
            [],
            8 * COUNT * CAP * owned * columns,
        )
    )


def solution(mesh):
    placed = (
        P(AXES, None, None),
        P(AXES, None, None),
        P(AXES, None, None),
        P(),
        P(AXES, None),
        P(AXES, None),
        P(AXES, None),
        P(AXES, None),
    )
    return jax.shard_map(
        solve,
        mesh=mesh,
        in_specs=placed,
        out_specs=(P(AXES, None), P(AXES, None)),
        check_vma=False,
    )
```
